32 devices in a mesh: real: 4 (over y, core), sky: 8 (over z, x).
Axes of the slice: x: 2, y: 2, z: 4, core: 2. Of those that a mesh axis runs over, the one named last changes fastest.
Arguments:
- potential_stock: bfloat16 [8, 256, 16384], P('real', 'sky'), may hold values from -6 to 6
- plane_pick: int32 [4], replicated, may hold values from 0 to 7, as said below
- col_shift: int32 [4, 4], P('real'), may hold values from 0 to 16383
- mirror: int32 [4, 4], P('real'), may hold values from 0 to 1
- subcell: int32 [32, 16], P('sky'), may hold values from 0 to 15
- lens_weight: float32 [4], replicated, may hold values from 0.02 to 0.08
Outputs:
- deflect: float32 [2, 4, 256, 2048], P(None, 'real', 'sky')
- distort: float32 [4, 4, 256, 2048], P(None, 'real', 'sky')
The draws below stay inside these ranges and needn't reach their ends.
Inputs may be any that keep to these rules, and one draw needn't show every extreme that they name: `plane_pick`: the 4 entries are distinct stored entries; entry q is held by the realization group q // 2.
All inputs are finite; a program needn't handle non-finite values.
Results may differ from the reference program's by a relative error of at most 0.0003.
Values may be sent and summed in bfloat16 or wider, within the bound.
A program may use at most 64 MiB of HBM per device.

```python
import math
import jax
import jax.numpy as jnp
from jax import lax

COLS = 2048
PLANE_COLS = 16384
PLANES = 4
SUB = 4
TILE_R = 8
TILE_C = 128
WIN_ROWS = 256
STOCK = 8
N_REAL = 4


def draw_plane_pick(key, part):
    first_key = jax.random.fold_in(key, 11)
    second_key = jax.random.fold_in(key, 23)
    middle = jax.random.permutation(first_key, STOCK - 2)[:PLANES - 2] + 1
    chosen = jnp.concatenate([jnp.array([0, STOCK - 1], jnp.int32), middle.astype(jnp.int32)])
    order = jax.random.permutation(second_key, PLANES)
    return chosen[order].astype(jnp.int32)


def touch_ends(values, rng, low, largest):
    shape = values.shape
    place = [jax.random.randint(jax.random.fold_in(rng, axis), (), 0, shape[axis]) for axis in range(len(shape))]
    values = values.at[tuple(place)].set(low)
    longest = shape.index(max(shape))
    place[longest] = (place[longest] + 1) % shape[longest]
    return values.at[tuple(place)].set(largest)


def block_levels(stream_key, shape, split, least, largest):
    gain = 1.0
    for position, blocks in split:
        draws = jax.random.uniform(jax.random.fold_in(jax.random.fold_in(stream_key, 6), position), (blocks,), jnp.float32, least / len(split), largest / len(split))
        gain = gain * jnp.repeat(jnp.exp(draws), shape[position] // blocks).reshape((-1,) + (1,) * (len(shape) - 1 - position))
    return gain


def scatter_about(rng, extent, spread, reach, split=(), held_as=jnp.bfloat16):
    factor_of = block_levels(rng, extent, split, -0.22, 0.18) if split else 1.0
    values = jax.random.normal(rng, extent, jnp.float32) * spread * factor_of
    return jnp.minimum(jnp.maximum(values, -reach), reach).astype(held_as)


def setup_inputs(seed: int = 0) -> dict:
    key_list = jax.random.split(jax.random.key(seed), 7)
    return {
        "potential_stock": scatter_about(key_list[0], (STOCK, WIN_ROWS, PLANE_COLS), 1.0, 6.0, ((0, 4), (1, 8))),
        "plane_pick": draw_plane_pick(jax.random.fold_in(key_list[6], 71), 0),
        "col_shift": touch_ends(jax.random.randint(key_list[2], (N_REAL, PLANES), 0, PLANE_COLS), jax.random.fold_in(key_list[2], 1), 0, PLANE_COLS - 1).astype(jnp.int32),
        "mirror": touch_ends(jax.random.randint(key_list[3], (N_REAL, PLANES), 0, 2), jax.random.fold_in(key_list[3], 1), 0, 1).astype(jnp.int32),
        "subcell": touch_ends(jax.random.randint(key_list[4], (WIN_ROWS // TILE_R, COLS // TILE_C), 0, SUB * SUB), jax.random.fold_in(key_list[4], 1), 0, (SUB * SUB) - 1).astype(jnp.int32),
        "lens_weight": jnp.clip(jnp.exp(jax.random.uniform(key_list[5], (PLANES,), jnp.float32, math.log(0.02), math.log(0.08))), 0.02, 0.08),
    }


first_coef = (1.0 / 12.0, -8.0 / 12.0, 0.0, 8.0 / 12.0, -1.0 / 12.0)
second_coef = (-1.0 / 12.0, 16.0 / 12.0, -30.0 / 12.0, 16.0 / 12.0, -1.0 / 12.0)


def cubic_weights(frac):
    sq = frac * frac
    cube = sq * frac
    return ((-cube + 2.0 * sq - frac) * 0.5, (3.0 * cube - 5.0 * sq + 2.0) * 0.5,
            (-3.0 * cube + 4.0 * sq + frac) * 0.5, (cube - sq) * 0.5)


def tap_weights(subcell):
    frac_x = ((subcell % SUB).astype(jnp.float32) + 0.5) / SUB
    frac_y = ((subcell // SUB).astype(jnp.float32) + 0.5) / SUB
    weights_x = tuple(w[:, None, :, None] for w in cubic_weights(frac_x))
    weights_y = tuple(w[:, None, :, None] for w in cubic_weights(frac_y))
    return weights_x, weights_y


def derivatives(tile):
    nrows = tile.shape[0] - 5
    ncols = tile.shape[1] - 5

    def window(drow, dcol):
        return tile[3 + drow:3 + drow + nrows, 3 + dcol:3 + dcol + ncols]

    grad_x = sum(first_coef[q] * window(0, q - 2) for q in range(5) if q != 2)
    grad_y = sum(first_coef[q] * window(q - 2, 0) for q in range(5) if q != 2)
    hess_xx = sum(second_coef[q] * window(0, q - 2) for q in range(5))
    hess_yy = sum(second_coef[q] * window(q - 2, 0) for q in range(5))
    hess_xy = sum(first_coef[p] * first_coef[q] * window(p - 2, q - 2)
                  for p in range(5) for q in range(5) if p != 2 and q != 2)
    return grad_x, grad_y, hess_xx, hess_yy, hess_xy


def sample(field, weights_x, weights_y, nrows, ncols):
    total = jnp.zeros((nrows // TILE_R, TILE_R, ncols // TILE_C, TILE_C), jnp.float32)
    for brow in range(4):
        inner = jnp.zeros_like(total)
        for acol in range(4):
            piece = field[brow:brow + nrows, acol:acol + ncols]
            piece = piece.reshape(nrows // TILE_R, TILE_R, ncols // TILE_C, TILE_C)
            inner = inner + weights_x[acol] * piece
        total = total + weights_y[brow] * inner
    return total.reshape(nrows, ncols)


def advance(state, tile, weights_x, weights_y, lens):
    nrows = tile.shape[0] - 8
    ncols = tile.shape[1] - 8
    fields = derivatives(tile.astype(jnp.float32))
    grad_x, grad_y, hess_xx, hess_yy, hess_xy = [sample(f, weights_x, weights_y, nrows, ncols) for f in fields]
    shift_x, shift_y, a_11, a_12, a_21, a_22 = state
    shift_x = shift_x + lens * grad_x
    shift_y = shift_y + lens * grad_y
    new_11 = a_11 - lens * (hess_xx * a_11 + hess_xy * a_21)
    new_12 = a_12 - lens * (hess_xx * a_12 + hess_xy * a_22)
    new_21 = a_21 - lens * (hess_xy * a_11 + hess_yy * a_21)
    new_22 = a_22 - lens * (hess_xy * a_12 + hess_yy * a_22)
    return (shift_x, shift_y, new_11, new_12, new_21, new_22)


def reference(potential_stock, plane_pick, col_shift, mirror, subcell, lens_weight):
    weights_x, weights_y = tap_weights(subcell)
    offsets = jnp.arange(-4, COLS + 4, dtype=jnp.int32)

    def trace_one(pair):
        shift_row, mirror_row = pair
        zeros = jnp.zeros((WIN_ROWS, COLS), jnp.float32)
        ones = jnp.ones((WIN_ROWS, COLS), jnp.float32)
        state = (zeros, zeros, ones, zeros, zeros, ones)
        for plane in range(PLANES):
            band = potential_stock[plane_pick[plane]]
            flipped = jnp.where(mirror_row[plane] == 1, band[:, ::-1], band)
            columns = ((shift_row[plane] + offsets) % PLANE_COLS).astype(jnp.int32)
            view = jnp.take(flipped, columns, axis=1)
            view = jnp.concatenate([view[-4:], view, view[:4]], axis=0)
            state = advance(state, view, weights_x, weights_y, lens_weight[plane])
        return state

    result = lax.map(trace_one, (col_shift, mirror))
    deflect = jnp.stack([result[0], result[1]])
    distort = jnp.stack([result[2], result[3], result[4], result[5]])
    return deflect, distort
```

```python
import functools

import jax
import jax.numpy as jnp
from jax import lax
from jax.experimental import pallas as pl
from jax.experimental.pallas import tpu as pltpu
from jax.sharding import PartitionSpec as P

SUB = 4
TILE_R = 8
TILE_C = 128
EDGE = 4
MESH = pl.DeviceIdType.MESH

first_coef = (1.0 / 12.0, -8.0 / 12.0, 0.0, 8.0 / 12.0, -1.0 / 12.0)
second_coef = (-1.0 / 12.0, 16.0 / 12.0, -30.0 / 12.0, 16.0 / 12.0, -1.0 / 12.0)


def cubic(t):
    return (
        (-(t**3) + 2 * t**2 - t) / 2,
        (3 * t**3 - 5 * t**2 + 2) / 2,
        (-3 * t**3 + 4 * t**2 + t) / 2,
        (t**3 - t**2) / 2,
    )


def convolved(taps, coef):
    out = [0.0] * 8
    for a, w in enumerate(taps):
        for q, c in enumerate(coef):
            out[a + q] += w * c
    return out


def filter_table():
    rows = []
    for o in range(SUB):
        taps = cubic((o + 0.5) / SUB)
        rows.append(list(taps) + convolved(taps, first_coef) + convolved(taps, second_coef))
    return rows


TABLE = filter_table()
NTAB = 20


def exchange_kernel(
    stock_ref, pick_ref, shift_ref, mirror_ref,
    main_ref, before_ref, after_ref,
    stock_t, tiles, send, edge32, esend, shifts_v, mirrors_v, shifts, mirrors,
    meta_send, meta_recv, local_sem, stock_sem, main_send, main_recv, edge_send, edge_recv,
):
    held, rows, cols = stock_ref.shape
    ntiles = cols // TILE_C
    out_tiles = main_ref.shape[2] // rows
    planes = pick_ref.shape[0]
    peers = lax.axis_size("real")
    strips = lax.axis_size("sky")
    me = lax.axis_index("real")
    strip = lax.axis_index("sky")
    above = lax.rem(strip + strips - 1, strips)
    below = lax.rem(strip + 1, strips)

    for e in range(held):
        @pl.loop(0, ntiles)
        def _(t):
            at = pl.ds(pl.multiple_of(t * TILE_C, TILE_C), TILE_C)
            pltpu.make_async_copy(
                stock_ref.at[e, :, at], stock_t.at[e * ntiles + t], stock_sem).start()

    barrier = pltpu.get_barrier_semaphore()
    for off in range(peers):
        r = lax.rem(me + off, peers)
        for s in (strip, above, below):
            if off == 0 and s is strip:
                continue
            pl.semaphore_signal(barrier, inc=1, device_id=(r, s), device_id_type=MESH)
    pl.semaphore_wait(barrier, 3 * peers - 1)

    def meta_copies(off):
        to = lax.rem(me + off, peers)
        return [
            pltpu.make_async_remote_copy(
                src_ref=src, dst_ref=dst.at[me], send_sem=meta_send.at[q, off],
                recv_sem=meta_recv.at[q, off], device_id=(to, strip), device_id_type=MESH)
            for q, (src, dst) in enumerate(((shift_ref, shifts_v), (mirror_ref, mirrors_v)))
        ]

    for off in range(1, peers):
        for copy in meta_copies(off):
            copy.start()
    own = [pltpu.make_async_copy(src, dst.at[me], local_sem.at[q])
           for q, (src, dst) in enumerate(((shift_ref, shifts_v), (mirror_ref, mirrors_v)))]
    for copy in own:
        copy.start()
    for copy in own:
        copy.wait()
    for off in range(1, peers):
        for copy in meta_copies(off):
            copy.wait()
    down = [pltpu.make_async_copy(src, dst, local_sem.at[q])
            for q, (src, dst) in enumerate(((shifts_v, shifts), (mirrors_v, mirrors)))]
    for copy in down:
        copy.start()
    for copy in down:
        copy.wait()

    lane_in = lax.broadcasted_iota(jnp.int32, (2 * TILE_C, TILE_C), 0)
    lane_out = lax.broadcasted_iota(jnp.int32, (2 * TILE_C, TILE_C), 1)

    def main_copy(off):
        to = lax.rem(me + off, peers)
        return pltpu.make_async_remote_copy(
            src_ref=send.at[off], dst_ref=main_ref.at[me], send_sem=main_send.at[off],
            recv_sem=main_recv.at[off], device_id=(to, strip), device_id_type=MESH)

    def edge_copies(off):
        to = lax.rem(me + off, peers)
        return [
            pltpu.make_async_remote_copy(
                src_ref=esend.at[off, 0], dst_ref=after_ref.at[me], send_sem=edge_send.at[0, off],
                recv_sem=edge_recv.at[0, off], device_id=(to, above), device_id_type=MESH),
            pltpu.make_async_remote_copy(
                src_ref=esend.at[off, 1], dst_ref=before_ref.at[me], send_sem=edge_send.at[1, off],
                recv_sem=edge_recv.at[1, off], device_id=(to, below), device_id_type=MESH),
        ]

    def cut(off):
        to = lax.rem(me + off, peers)
        for e in range(held):
            q = me * held + e
            shift = jnp.int32(0)
            turned = jnp.int32(0)
            for k in range(planes):
                hit = pick_ref[k] == q
                shift = jnp.where(hit, shifts[to, 0, k], shift)
                turned = jnp.where(hit, mirrors[to, 0, k], turned)
            step = 1 - 2 * turned
            start = turned * (cols + EDGE - 1 - shift) + (1 - turned) * (shift + cols - EDGE)
            start = lax.rem(start, cols)
            base = lax.div(start, TILE_C)
            inner = start - base * TILE_C
            for u in range(out_tiles + 1):
                at = e * ntiles + lax.rem(base + step * u + ntiles, ntiles)
                tiles[u * rows:(u + 1) * rows, :] = stock_t[at]
            near = lane_in == inner + step * lane_out
            far = lane_in - TILE_C == inner + step * (lane_out - TILE_C)
            choose = ((near & (lane_in < TILE_C)) | (far & (lane_in >= TILE_C)))
            choose = choose.astype(jnp.float32).astype(jnp.bfloat16)
            n = out_tiles * rows
            pairs = jnp.concatenate([tiles[0:n, :], tiles[rows:n + rows, :]], axis=1)
            view = jnp.dot(pairs, choose, preferred_element_type=jnp.float32)
            send[off, e] = view.astype(jnp.bfloat16)
            for t in range(out_tiles):
                edge32[0, t * EDGE:(t + 1) * EDGE, :] = view[t * rows:t * rows + EDGE, :]
                edge32[1, t * EDGE:(t + 1) * EDGE, :] = view[(t + 1) * rows - EDGE:(t + 1) * rows, :]
            esend[off, 0, e] = edge32[0].astype(jnp.bfloat16)
            esend[off, 1, e] = edge32[1].astype(jnp.bfloat16)

    pltpu.make_async_copy(stock_t, stock_t, stock_sem).wait()
    edge32[...] = jnp.zeros_like(edge32)
    order = sorted(range(1, peers), key=lambda off: abs(2 * off - peers)) + [0]
    for off in order:
        cut(off)
        if off:
            main_copy(off).start()
        else:
            keep = pltpu.make_async_copy(send.at[0], main_ref.at[me], local_sem.at[0])
            keep.start()
        for copy in edge_copies(off):
            copy.start()
    keep.wait()
    for off in order:
        if off:
            main_copy(off).wait()
        for copy in edge_copies(off):
            copy.wait()


def trace_kernel(
    pick_ref, subcell_ref, lens_ref, main_ref, before_ref, after_ref,
    deflect_ref, distort_ref,
    main_v, before_v, after_v, view, table, sems,
):
    planes = pick_ref.shape[0]
    held = main_ref.shape[1]
    nrows = deflect_ref.shape[2]
    ncols = deflect_ref.shape[3]
    out_tiles = main_v.shape[1] // nrows

    copies = []
    for k in range(planes):
        group = pick_ref[k] // held
        e = lax.rem(pick_ref[k], held)
        copies.append([
            pltpu.make_async_copy(src.at[group, e], dst.at[k], sems.at[k, q])
            for q, (src, dst) in enumerate(
                ((main_ref, main_v), (before_ref, before_v), (after_ref, after_v)))
        ])
        for copy in copies[k]:
            copy.start()
    for o in range(SUB):
        for m in range(NTAB):
            table[o, m] = jnp.float32(TABLE[o][m])
    for k in range(planes):
        for copy in copies[k]:
            copy.wait()
        up = before_v[k].astype(jnp.float32)
        down = after_v[k].astype(jnp.float32)
        for t in range(out_tiles):
            view[k, t, TILE_R:TILE_R + nrows, :] = main_v[k, t * nrows:(t + 1) * nrows, :].astype(jnp.float32)
            view[k, t, TILE_R - EDGE:TILE_R, :] = up[t * EDGE:(t + 1) * EDGE]
            view[k, t, TILE_R + nrows:TILE_R + nrows + EDGE, :] = down[t * EDGE:(t + 1) * EDGE]

    def tile(i, j):
        o = subcell_ref[i, j]
        oy = o // SUB
        ox = o - oy * SUB
        wx = [table[ox, m] for m in range(NTAB)]
        wy = [table[oy, m] for m in range(NTAB)]
        x0, x1, x2 = wx[:4], wx[4:12], wx[12:20]
        y0, y1, y2 = wy[:4], wy[4:12], wy[12:20]
        shape = (TILE_R, TILE_C)
        zero = jnp.zeros(shape, jnp.float32)
        one = jnp.ones(shape, jnp.float32)
        dx, dy, a11, a12, a21, a22 = zero, zero, one, zero, zero, one
        for k in range(planes):
            parts = []
            for side in range(2):
                v = [view[k, j + side, pl.ds(TILE_R + i * TILE_R + n, TILE_R), :] for n in range(-3, 5)]
                parts.append((
                    sum(y0[b] * v[b + 2] for b in range(4)),
                    sum(y1[b] * v[b] for b in range(8)),
                    sum(y2[b] * v[b] for b in range(8)),
                ))
            f0, f1, f2 = [jnp.concatenate([parts[0][q], parts[1][q]], axis=1) for q in range(3)]
            s0 = [f0[:, m + 1:m + 1 + TILE_C] for m in range(8)]
            s1 = [f1[:, m + 1:m + 1 + TILE_C] for m in range(8)]
            s2 = [f2[:, m + 3:m + 3 + TILE_C] for m in range(4)]
            gx = sum(x1[m] * s0[m] for m in range(8))
            xx = sum(x2[m] * s0[m] for m in range(8))
            xy = sum(x1[m] * s1[m] for m in range(8))
            gy = sum(x0[m] * s1[m + 2] for m in range(4))
            yy = sum(x0[m] * s2[m] for m in range(4))
            lens = lens_ref[k]
            dx = dx + lens * gx
            dy = dy + lens * gy
            xx, xy, yy = lens * xx, lens * xy, lens * yy
            a11, a12, a21, a22 = (
                a11 - (xx * a11 + xy * a21),
                a12 - (xx * a12 + xy * a22),
                a21 - (xy * a11 + yy * a21),
                a22 - (xy * a12 + yy * a22),
            )
        at = pl.ds(pl.multiple_of(j * TILE_C, TILE_C), TILE_C)
        rs = slice(i * TILE_R, (i + 1) * TILE_R)
        deflect_ref[0, 0, rs, at] = dx
        deflect_ref[1, 0, rs, at] = dy
        for n, a in enumerate((a11, a12, a21, a22)):
            distort_ref[n, 0, rs, at] = a

    @pl.loop(0, ncols // TILE_C)
    def _(j):
        for i in range(nrows // TILE_R):
            tile(i, j)


def body(potential_stock, plane_pick, col_shift, mirror, subcell, lens_weight):
    held, rows, cols = potential_stock.shape
    peers = lax.axis_size("real")
    planes = plane_pick.shape[0]
    ncols = subcell.shape[1] * TILE_C
    out_tiles = -(-(ncols + 2 * EDGE) // TILE_C)
    erows = -(-(out_tiles * EDGE) // 16) * 16
    n = out_tiles * rows
    vm = pl.BlockSpec(memory_space=pltpu.VMEM)
    sm = pl.BlockSpec(memory_space=pltpu.SMEM)
    anyw = pl.BlockSpec(memory_space=pl.ANY)
    bf = jnp.bfloat16
    dma = pltpu.SemaphoreType.DMA
    main, before, after = pl.pallas_call(
        exchange_kernel,
        out_shape=(
            jax.ShapeDtypeStruct((peers, held, n, TILE_C), bf),
            jax.ShapeDtypeStruct((peers, held, erows, TILE_C), bf),
            jax.ShapeDtypeStruct((peers, held, erows, TILE_C), bf),
        ),
        in_specs=[anyw, sm, vm, vm],
        out_specs=(anyw, anyw, anyw),
        scratch_shapes=[
            pltpu.VMEM((held * (cols // TILE_C), rows, TILE_C), bf),
            pltpu.VMEM((n + rows, TILE_C), bf),
            pltpu.VMEM((peers, held, n, TILE_C), bf),
            pltpu.VMEM((2, erows, TILE_C), jnp.float32),
            pltpu.VMEM((peers, 2, held, erows, TILE_C), bf),
            pltpu.VMEM((peers, 1, planes), jnp.int32),
            pltpu.VMEM((peers, 1, planes), jnp.int32),
            pltpu.SMEM((peers, 1, planes), jnp.int32),
            pltpu.SMEM((peers, 1, planes), jnp.int32),
            dma((2, peers)), dma((2, peers)), dma((2,)), dma,
            dma((peers,)), dma((peers,)), dma((2, peers)), dma((2, peers)),
        ],
        compiler_params=pltpu.CompilerParams(collective_id=0, has_side_effects=True),
        name="exchange",
    )(potential_stock, plane_pick, col_shift, mirror)
    f32 = jnp.float32
    nrows = subcell.shape[0] * TILE_R
    return pl.pallas_call(
        trace_kernel,
        out_shape=(
            jax.ShapeDtypeStruct((2, 1, nrows, ncols), f32),
            jax.ShapeDtypeStruct((4, 1, nrows, ncols), f32),
        ),
        in_specs=[sm, sm, sm, anyw, anyw, anyw],
        out_specs=(vm, vm),
        scratch_shapes=[
            pltpu.VMEM((planes, n, TILE_C), bf),
            pltpu.VMEM((planes, erows, TILE_C), bf),
            pltpu.VMEM((planes, erows, TILE_C), bf),
            pltpu.VMEM((planes, out_tiles, nrows + 2 * TILE_R, TILE_C), f32),
            pltpu.SMEM((SUB, NTAB), f32),
            dma((planes, 3)),
        ],
        name="trace",
    )(plane_pick, subcell, lens_weight, main, before, after)


def solution(mesh):
    return jax.shard_map(
        body,
        mesh=mesh,
        in_specs=(
            P("real", "sky", None),
            P(),
            P("real", None),
            P("real", None),
            P("sky", None),
            P(),
        ),
        out_specs=(P(None, "real", "sky", None), P(None, "real", "sky", None)),
        check_vma=False,
    )
```

```python
import jax
import jax.numpy as jnp
import numpy as np
from jax import lax
from jax.experimental import pallas as pl
from jax.experimental.pallas import tpu as pltpu
from jax.sharding import PartitionSpec as P

SUB = 4
TILE_R = 8
TILE_C = 128
EDGE = 4
MESH = pl.DeviceIdType.MESH

first_coef = (1.0 / 12.0, -8.0 / 12.0, 0.0, 8.0 / 12.0, -1.0 / 12.0)
second_coef = (-1.0 / 12.0, 16.0 / 12.0, -30.0 / 12.0, 16.0 / 12.0, -1.0 / 12.0)


def cubic(t):
    return (
        (-(t**3) + 2 * t**2 - t) / 2,
        (3 * t**3 - 5 * t**2 + 2) / 2,
        (-3 * t**3 + 4 * t**2 + t) / 2,
        (t**3 - t**2) / 2,
    )


def convolved(taps, coef):
    out = [0.0] * 8
    for a, w in enumerate(taps):
        for q, c in enumerate(coef):
            out[a + q] += w * c
    return out


def filter_table():
    rows = []
    for o in range(SUB):
        taps = cubic((o + 0.5) / SUB)
        rows.append(list(taps) + convolved(taps, first_coef) + convolved(taps, second_coef))
    return rows


TABLE = filter_table()
NTAB = 20
X_SCALE = 12288.0


def column_filters():
    full = np.zeros((2 * TILE_C, SUB, 3, TILE_C))
    out = np.arange(TILE_C)
    for o, row in enumerate(TABLE):
        for m in range(4):
            full[out + 3 + m, o, 0, out] = row[m] * X_SCALE
        for m in range(8):
            full[out + 1 + m, o, 1, out] = row[4 + m] * X_SCALE
            full[out + 1 + m, o, 2, out] = row[12 + m] * X_SCALE
    full = np.rint(full.reshape(2 * TILE_C, SUB * 3 * TILE_C)).astype(np.float32)
    high = full.astype(jnp.bfloat16)
    low = (full - high.astype(np.float32)).astype(jnp.bfloat16)
    return np.concatenate([high, low], axis=0)


def exchange_kernel(
    stock_ref, pick_ref, shift_ref, mirror_ref,
    main_ref, before_ref, after_ref,
    stock_t, tiles, send, edge32, esend, shifts_v, mirrors_v, shifts, mirrors,
    meta_send, meta_recv, local_sem, stock_sem, main_send, main_recv, edge_send, edge_recv,
):
    held, rows, cols = stock_ref.shape
    ntiles = cols // TILE_C
    out_tiles = main_ref.shape[2] // rows
    planes = pick_ref.shape[0]
    peers = lax.axis_size("real")
    strips = lax.axis_size("sky")
    me = lax.axis_index("real")
    strip = lax.axis_index("sky")
    above = lax.rem(strip + strips - 1, strips)
    below = lax.rem(strip + 1, strips)

    for e in range(held):
        @pl.loop(0, ntiles)
        def _(t):
            at = pl.ds(pl.multiple_of(t * TILE_C, TILE_C), TILE_C)
            pltpu.make_async_copy(
                stock_ref.at[e, :, at], stock_t.at[e * ntiles + t], stock_sem).start()

    barrier = pltpu.get_barrier_semaphore()
    for off in range(peers):
        r = lax.rem(me + off, peers)
        for s in (strip, above, below):
            if off == 0 and s is strip:
                continue
            pl.semaphore_signal(barrier, inc=1, device_id=(r, s), device_id_type=MESH)
    pl.semaphore_wait(barrier, 3 * peers - 1)

    def meta_copies(off):
        to = lax.rem(me + off, peers)
        return [
            pltpu.make_async_remote_copy(
                src_ref=src, dst_ref=dst.at[me], send_sem=meta_send.at[q, off],
                recv_sem=meta_recv.at[q, off], device_id=(to, strip), device_id_type=MESH)
            for q, (src, dst) in enumerate(((shift_ref, shifts_v), (mirror_ref, mirrors_v)))
        ]

    for off in range(1, peers):
        for copy in meta_copies(off):
            copy.start()
    own = [pltpu.make_async_copy(src, dst.at[me], local_sem.at[q])
           for q, (src, dst) in enumerate(((shift_ref, shifts_v), (mirror_ref, mirrors_v)))]
    for copy in own:
        copy.start()
    for copy in own:
        copy.wait()
    for off in range(1, peers):
        for copy in meta_copies(off):
            copy.wait()
    down = [pltpu.make_async_copy(src, dst, local_sem.at[q])
            for q, (src, dst) in enumerate(((shifts_v, shifts), (mirrors_v, mirrors)))]
    for copy in down:
        copy.start()
    for copy in down:
        copy.wait()

    lane_in = lax.broadcasted_iota(jnp.int32, (2 * TILE_C, TILE_C), 0)
    lane_out = lax.broadcasted_iota(jnp.int32, (2 * TILE_C, TILE_C), 1)

    def main_copy(off):
        to = lax.rem(me + off, peers)
        return pltpu.make_async_remote_copy(
            src_ref=send.at[off], dst_ref=main_ref.at[me], send_sem=main_send.at[off],
            recv_sem=main_recv.at[off], device_id=(to, strip), device_id_type=MESH)

    def edge_copies(off):
        to = lax.rem(me + off, peers)
        return [
            pltpu.make_async_remote_copy(
                src_ref=esend.at[off, 0], dst_ref=after_ref.at[me], send_sem=edge_send.at[0, off],
                recv_sem=edge_recv.at[0, off], device_id=(to, above), device_id_type=MESH),
            pltpu.make_async_remote_copy(
                src_ref=esend.at[off, 1], dst_ref=before_ref.at[me], send_sem=edge_send.at[1, off],
                recv_sem=edge_recv.at[1, off], device_id=(to, below), device_id_type=MESH),
        ]

    def cut(off):
        to = lax.rem(me + off, peers)
        for e in range(held):
            q = me * held + e
            shift = jnp.int32(0)
            turned = jnp.int32(0)
            for k in range(planes):
                hit = pick_ref[k] == q
                shift = jnp.where(hit, shifts[to, 0, k], shift)
                turned = jnp.where(hit, mirrors[to, 0, k], turned)
            step = 1 - 2 * turned
            start = turned * (cols + EDGE - 1 - shift) + (1 - turned) * (shift + cols - EDGE)
            start = lax.rem(start, cols)
            base = lax.div(start, TILE_C)
            inner = start - base * TILE_C
            for u in range(out_tiles + 1):
                at = e * ntiles + lax.rem(base + step * u + ntiles, ntiles)
                tiles[u * rows:(u + 1) * rows, :] = stock_t[at]
            near = lane_in == inner + step * lane_out
            far = lane_in - TILE_C == inner + step * (lane_out - TILE_C)
            choose = ((near & (lane_in < TILE_C)) | (far & (lane_in >= TILE_C)))
            choose = choose.astype(jnp.float32).astype(jnp.bfloat16)
            n = out_tiles * rows
            pairs = jnp.concatenate([tiles[0:n, :], tiles[rows:n + rows, :]], axis=1)
            view = jnp.dot(pairs, choose, preferred_element_type=jnp.float32)
            send[off, e] = view.astype(jnp.bfloat16)
            for t in range(out_tiles):
                edge32[0, t * EDGE:(t + 1) * EDGE, :] = view[t * rows:t * rows + EDGE, :]
                edge32[1, t * EDGE:(t + 1) * EDGE, :] = view[(t + 1) * rows - EDGE:(t + 1) * rows, :]
            esend[off, 0, e] = edge32[0].astype(jnp.bfloat16)
            esend[off, 1, e] = edge32[1].astype(jnp.bfloat16)

    pltpu.make_async_copy(stock_t, stock_t, stock_sem).wait()
    edge32[...] = jnp.zeros_like(edge32)
    order = sorted(range(1, peers), key=lambda off: abs(2 * off - peers)) + [0]
    for off in order:
        cut(off)
        if off:
            main_copy(off).start()
        else:
            keep = pltpu.make_async_copy(send.at[0], main_ref.at[me], local_sem.at[0])
            keep.start()
        for copy in edge_copies(off):
            copy.start()
    keep.wait()
    for off in order:
        if off:
            main_copy(off).wait()
        for copy in edge_copies(off):
            copy.wait()


def trace_kernel(
    pick_ref, subcell_ref, lens_ref, filt_ref, main_ref, before_ref, after_ref,
    deflect_ref, distort_ref,
    main_v, before_v, after_v, filt_v, edges, field, table, sems, filt_sem,
):
    planes = pick_ref.shape[0]
    held = main_ref.shape[1]
    nrows = deflect_ref.shape[2]
    ncols = deflect_ref.shape[3]
    tiles = ncols // TILE_C
    nfilt = filt_ref.shape[1] // TILE_C

    filt_copy = pltpu.make_async_copy(filt_ref, filt_v, filt_sem)
    filt_copy.start()
    copies = []
    for k in range(planes):
        group = pick_ref[k] // held
        e = lax.rem(pick_ref[k], held)
        copies.append([
            pltpu.make_async_copy(src.at[group, e], dst.at[k], sems.at[k, q])
            for q, (src, dst) in enumerate(
                ((main_ref, main_v), (before_ref, before_v), (after_ref, after_v)))
        ])
        for copy in copies[k]:
            copy.start()
    for o in range(SUB):
        for m in range(NTAB):
            table[o, m] = jnp.float32(TABLE[o][m] / X_SCALE)
    for k in range(planes):
        for copy in copies[k]:
            copy.wait()
    for k in range(planes):
        up = before_v[k].astype(jnp.float32)
        down = after_v[k].astype(jnp.float32)
        for t in range(tiles + 1):
            edges[k, t, EDGE:2 * EDGE, :] = up[t * EDGE:(t + 1) * EDGE]
            edges[k, t, 0:EDGE, :] = down[t * EDGE:(t + 1) * EDGE]
    filt_copy.wait()

    @pl.loop(0, planes)
    def _(k):
        m = tiles * nrows
        flank = edges[k]
        near = jnp.concatenate(
            [main_v[k, 0:m, :], flank[0:tiles].reshape(tiles * TILE_R, TILE_C).astype(jnp.bfloat16)], axis=0)
        far = jnp.concatenate(
            [main_v[k, nrows:m + nrows, :], flank[1:tiles + 1].reshape(tiles * TILE_R, TILE_C).astype(jnp.bfloat16)],
            axis=0)
        lhs = jnp.concatenate([near, far, near, far], axis=1)
        for c in range(0, nfilt, 2):
            got = jnp.dot(lhs, filt_v[:, c * TILE_C:(c + 2) * TILE_C], preferred_element_type=jnp.float32)
            for h in range(2):
                part = got[:, h * TILE_C:(h + 1) * TILE_C]
                ends = part[m:].reshape(tiles, TILE_R, TILE_C)
                field[c + h, k, :, TILE_R:TILE_R + nrows, :] = part[:m].reshape(tiles, nrows, TILE_C)
                field[c + h, k, :, 0:TILE_R, :] = ends
                field[c + h, k, :, TILE_R + nrows:2 * TILE_R + nrows, :] = ends

    def tile(i, j):
        o = subcell_ref[i, j]
        oy = o // SUB
        fx = (o - oy * SUB) * 3
        wy = [table[oy, m] for m in range(NTAB)]
        y0, y1, y2 = wy[:4], wy[4:12], wy[12:20]
        shape = (TILE_R, TILE_C)
        zero = jnp.zeros(shape, jnp.float32)
        one = jnp.ones(shape, jnp.float32)
        dx, dy, a11, a12, a21, a22 = zero, zero, one, zero, zero, one
        for k in range(planes):
            def row(q, n):
                return field[fx + q, k, j, pl.ds(TILE_R + i * TILE_R + n, TILE_R), :]
            plain = [row(0, n) for n in range(-3, 5)]
            slope = [row(1, n) for n in range(-3, 5)]
            curve = [row(2, n) for n in range(-1, 3)]
            gx = sum(y0[b] * slope[b + 2] for b in range(4))
            xx = sum(y0[b] * curve[b] for b in range(4))
            xy = sum(y1[b] * slope[b] for b in range(8))
            gy = sum(y1[b] * plain[b] for b in range(8))
            yy = sum(y2[b] * plain[b] for b in range(8))
            lens = lens_ref[k]
            dx = dx + lens * gx
            dy = dy + lens * gy
            xx, xy, yy = lens * xx, lens * xy, lens * yy
            a11, a12, a21, a22 = (
                a11 - (xx * a11 + xy * a21),
                a12 - (xx * a12 + xy * a22),
                a21 - (xy * a11 + yy * a21),
                a22 - (xy * a12 + yy * a22),
            )
        at = pl.ds(pl.multiple_of(j * TILE_C, TILE_C), TILE_C)
        rs = slice(i * TILE_R, (i + 1) * TILE_R)
        deflect_ref[0, 0, rs, at] = dx
        deflect_ref[1, 0, rs, at] = dy
        for n, a in enumerate((a11, a12, a21, a22)):
            distort_ref[n, 0, rs, at] = a

    @pl.loop(0, tiles)
    def _(j):
        for i in range(nrows // TILE_R):
            tile(i, j)


def body(potential_stock, plane_pick, col_shift, mirror, subcell, lens_weight):
    held, rows, cols = potential_stock.shape
    peers = lax.axis_size("real")
    planes = plane_pick.shape[0]
    ncols = subcell.shape[1] * TILE_C
    out_tiles = -(-(ncols + 2 * EDGE) // TILE_C)
    erows = -(-(out_tiles * EDGE) // 16) * 16
    n = out_tiles * rows
    vm = pl.BlockSpec(memory_space=pltpu.VMEM)
    sm = pl.BlockSpec(memory_space=pltpu.SMEM)
    anyw = pl.BlockSpec(memory_space=pl.ANY)
    bf = jnp.bfloat16
    dma = pltpu.SemaphoreType.DMA
    main, before, after = pl.pallas_call(
        exchange_kernel,
        out_shape=(
            jax.ShapeDtypeStruct((peers, held, n, TILE_C), bf),
            jax.ShapeDtypeStruct((peers, held, erows, TILE_C), bf),
            jax.ShapeDtypeStruct((peers, held, erows, TILE_C), bf),
        ),
        in_specs=[anyw, sm, vm, vm],
        out_specs=(anyw, anyw, anyw),
        scratch_shapes=[
            pltpu.VMEM((held * (cols // TILE_C), rows, TILE_C), bf),
            pltpu.VMEM((n + rows, TILE_C), bf),
            pltpu.VMEM((peers, held, n, TILE_C), bf),
            pltpu.VMEM((2, erows, TILE_C), jnp.float32),
            pltpu.VMEM((peers, 2, held, erows, TILE_C), bf),
            pltpu.VMEM((peers, 1, planes), jnp.int32),
            pltpu.VMEM((peers, 1, planes), jnp.int32),
            pltpu.SMEM((peers, 1, planes), jnp.int32),
            pltpu.SMEM((peers, 1, planes), jnp.int32),
            dma((2, peers)), dma((2, peers)), dma((2,)), dma,
            dma((peers,)), dma((peers,)), dma((2, peers)), dma((2, peers)),
        ],
        compiler_params=pltpu.CompilerParams(collective_id=0, has_side_effects=True),
        name="exchange",
    )(potential_stock, plane_pick, col_shift, mirror)
    f32 = jnp.float32
    nrows = subcell.shape[0] * TILE_R
    filt = jnp.asarray(column_filters())
    return pl.pallas_call(
        trace_kernel,
        out_shape=(
            jax.ShapeDtypeStruct((2, 1, nrows, ncols), f32),
            jax.ShapeDtypeStruct((4, 1, nrows, ncols), f32),
        ),
        in_specs=[sm, sm, sm, anyw, anyw, anyw, anyw],
        out_specs=(vm, vm),
        scratch_shapes=[
            pltpu.VMEM((planes, n, TILE_C), bf),
            pltpu.VMEM((planes, erows, TILE_C), bf),
            pltpu.VMEM((planes, erows, TILE_C), bf),
            pltpu.VMEM(filt.shape, bf),
            pltpu.VMEM((planes, ncols // TILE_C + 1, TILE_R, TILE_C), f32),
            pltpu.VMEM((SUB * 3, planes, ncols // TILE_C, nrows + 2 * TILE_R, TILE_C), f32),
            pltpu.SMEM((SUB, NTAB), f32),
            dma((planes, 3)), dma,
        ],
        name="trace",
    )(plane_pick, subcell, lens_weight, filt, main, before, after)


def solution(mesh):
    return jax.shard_map(
        body,
        mesh=mesh,
        in_specs=(
            P("real", "sky", None),
            P(),
            P("real", None),
            P("real", None),
            P("sky", None),
            P(),
        ),
        out_specs=(P(None, "real", "sky", None), P(None, "real", "sky", None)),
        check_vma=False,
    )
```

```python
import jax
import jax.numpy as jnp
import numpy as np
from jax import lax
from jax.experimental import pallas as pl
from jax.experimental.pallas import tpu as pltpu
from jax.sharding import PartitionSpec as P

SUB = 4
TILE_R = 8
TILE_C = 128
EDGE = 4
MESH = pl.DeviceIdType.MESH

first_coef = (1.0 / 12.0, -8.0 / 12.0, 0.0, 8.0 / 12.0, -1.0 / 12.0)
second_coef = (-1.0 / 12.0, 16.0 / 12.0, -30.0 / 12.0, 16.0 / 12.0, -1.0 / 12.0)


def cubic(t):
    return (
        (-(t**3) + 2 * t**2 - t) / 2,
        (3 * t**3 - 5 * t**2 + 2) / 2,
        (-3 * t**3 + 4 * t**2 + t) / 2,
        (t**3 - t**2) / 2,
    )


def convolved(taps, coef):
    out = [0.0] * 8
    for a, w in enumerate(taps):
        for q, c in enumerate(coef):
            out[a + q] += w * c
    return out


def filter_table():
    rows = []
    for o in range(SUB):
        taps = cubic((o + 0.5) / SUB)
        rows.append(list(taps) + convolved(taps, first_coef) + convolved(taps, second_coef))
    return rows


TABLE = filter_table()
NTAB = 20
X_SCALE = 12288.0


def column_filters():
    full = np.zeros((2 * TILE_C, SUB, 3, TILE_C))
    out = np.arange(TILE_C)
    for o, row in enumerate(TABLE):
        for m in range(4):
            full[out + 3 + m, o, 0, out] = row[m] * X_SCALE
        for m in range(8):
            full[out + 1 + m, o, 1, out] = row[4 + m] * X_SCALE
            full[out + 1 + m, o, 2, out] = row[12 + m] * X_SCALE
    full = np.rint(full.reshape(2 * TILE_C, SUB * 3 * TILE_C)).astype(np.float32)
    high = full.astype(jnp.bfloat16)
    low = (full - high.astype(np.float32)).astype(jnp.bfloat16)
    return np.concatenate([high, low], axis=0)


def exchange_kernel(
    stock_ref, pick_ref, shift_ref, mirror_ref,
    main_ref, before_ref, after_ref,
    stock_t, tiles, send, edge32, esend, shifts_v, mirrors_v, shifts, mirrors,
    meta_send, meta_recv, local_sem, stock_sem, main_send, main_recv, edge_send, edge_recv,
):
    held, blocks, ntiles = stock_ref.shape[:3]
    rows, cols = blocks * TILE_R, ntiles * TILE_C
    out_tiles = main_ref.shape[2] // rows
    planes = pick_ref.shape[0]
    peers = lax.axis_size("real")
    strips = lax.axis_size("sky")
    me = lax.axis_index("real")
    strip = lax.axis_index("sky")
    above = lax.rem(strip + strips - 1, strips)
    below = lax.rem(strip + 1, strips)

    stock_copy = pltpu.make_async_copy(stock_ref, stock_t, stock_sem)
    stock_copy.start()
    barrier = pltpu.get_barrier_semaphore()
    for off in range(peers):
        r = lax.rem(me + off, peers)
        for s in (strip, above, below):
            if off == 0 and s is strip:
                continue
            pl.semaphore_signal(barrier, inc=1, device_id=(r, s), device_id_type=MESH)
    pl.semaphore_wait(barrier, 3 * peers - 1)

    def meta_copies(off):
        to = lax.rem(me + off, peers)
        return [
            pltpu.make_async_remote_copy(
                src_ref=src, dst_ref=dst.at[me], send_sem=meta_send.at[q, off],
                recv_sem=meta_recv.at[q, off], device_id=(to, strip), device_id_type=MESH)
            for q, (src, dst) in enumerate(((shift_ref, shifts_v), (mirror_ref, mirrors_v)))
        ]

    for off in range(1, peers):
        for copy in meta_copies(off):
            copy.start()
    own = [pltpu.make_async_copy(src, dst.at[me], local_sem.at[q])
           for q, (src, dst) in enumerate(((shift_ref, shifts_v), (mirror_ref, mirrors_v)))]
    for copy in own:
        copy.start()
    for copy in own:
        copy.wait()
    for off in range(1, peers):
        for copy in meta_copies(off):
            copy.wait()
    down = [pltpu.make_async_copy(src, dst, local_sem.at[q])
            for q, (src, dst) in enumerate(((shifts_v, shifts), (mirrors_v, mirrors)))]
    for copy in down:
        copy.start()
    for copy in down:
        copy.wait()

    lane_in = lax.broadcasted_iota(jnp.int32, (2 * TILE_C, TILE_C), 0)
    lane_out = lax.broadcasted_iota(jnp.int32, (2 * TILE_C, TILE_C), 1)

    def main_copy(off):
        to = lax.rem(me + off, peers)
        return pltpu.make_async_remote_copy(
            src_ref=send.at[off], dst_ref=main_ref.at[me], send_sem=main_send.at[off],
            recv_sem=main_recv.at[off], device_id=(to, strip), device_id_type=MESH)

    def edge_copies(off):
        to = lax.rem(me + off, peers)
        return [
            pltpu.make_async_remote_copy(
                src_ref=esend.at[off, 0], dst_ref=after_ref.at[me], send_sem=edge_send.at[0, off],
                recv_sem=edge_recv.at[0, off], device_id=(to, above), device_id_type=MESH),
            pltpu.make_async_remote_copy(
                src_ref=esend.at[off, 1], dst_ref=before_ref.at[me], send_sem=edge_send.at[1, off],
                recv_sem=edge_recv.at[1, off], device_id=(to, below), device_id_type=MESH),
        ]

    def cut(off):
        to = lax.rem(me + off, peers)
        for e in range(held):
            q = me * held + e
            shift = jnp.int32(0)
            turned = jnp.int32(0)
            for k in range(planes):
                hit = pick_ref[k] == q
                shift = jnp.where(hit, shifts[to, 0, k], shift)
                turned = jnp.where(hit, mirrors[to, 0, k], turned)
            step = 1 - 2 * turned
            start = turned * (cols + EDGE - 1 - shift) + (1 - turned) * (shift + cols - EDGE)
            start = lax.rem(start, cols)
            base = lax.div(start, TILE_C)
            inner = start - base * TILE_C
            for u in range(out_tiles + 1):
                at = lax.rem(base + step * u + ntiles, ntiles)
                for b in range(blocks):
                    tiles[u * rows + b * TILE_R:u * rows + (b + 1) * TILE_R, :] = stock_t[e, b, at]
            near = lane_in == inner + step * lane_out
            far = lane_in - TILE_C == inner + step * (lane_out - TILE_C)
            choose = ((near & (lane_in < TILE_C)) | (far & (lane_in >= TILE_C)))
            choose = choose.astype(jnp.float32).astype(jnp.bfloat16)
            n = out_tiles * rows
            pairs = jnp.concatenate([tiles[0:n, :], tiles[rows:n + rows, :]], axis=1)
            view = jnp.dot(pairs, choose, preferred_element_type=jnp.float32)
            send[off, e] = view.astype(jnp.bfloat16)
            for t in range(out_tiles):
                edge32[0, t * EDGE:(t + 1) * EDGE, :] = view[t * rows:t * rows + EDGE, :]
                edge32[1, t * EDGE:(t + 1) * EDGE, :] = view[(t + 1) * rows - EDGE:(t + 1) * rows, :]
            esend[off, 0, e] = edge32[0].astype(jnp.bfloat16)
            esend[off, 1, e] = edge32[1].astype(jnp.bfloat16)

    stock_copy.wait()
    edge32[...] = jnp.zeros_like(edge32)
    order = sorted(range(1, peers), key=lambda off: abs(2 * off - peers)) + [0]
    for off in order:
        cut(off)
        if off:
            main_copy(off).start()
        else:
            keep = pltpu.make_async_copy(send.at[0], main_ref.at[me], local_sem.at[0])
            keep.start()
        for copy in edge_copies(off):
            copy.start()
    keep.wait()
    for off in order:
        if off:
            main_copy(off).wait()
        for copy in edge_copies(off):
            copy.wait()


def trace_kernel(
    pick_ref, subcell_ref, lens_ref, filt_ref, main_ref, before_ref, after_ref,
    deflect_ref, distort_ref,
    main_v, before_v, after_v, filt_v, edges, pairs, field, table, sems, filt_sem,
):
    planes = pick_ref.shape[0]
    held = main_ref.shape[1]
    nrows = deflect_ref.shape[2]
    ncols = deflect_ref.shape[3]
    tiles = ncols // TILE_C
    nfilt = filt_ref.shape[1] // TILE_C

    filt_copy = pltpu.make_async_copy(filt_ref, filt_v, filt_sem)
    filt_copy.start()
    copies = []
    for k in range(planes):
        group = pick_ref[k] // held
        e = lax.rem(pick_ref[k], held)
        copies.append([
            pltpu.make_async_copy(src.at[group, e], dst.at[k], sems.at[k, q])
            for q, (src, dst) in enumerate(
                ((main_ref, main_v), (before_ref, before_v), (after_ref, after_v)))
        ])
        for copy in copies[k]:
            copy.start()
    for o in range(SUB):
        for m in range(NTAB):
            table[o, m] = jnp.float32(TABLE[o][m] / X_SCALE)
    for k in range(planes):
        for copy in copies[k]:
            copy.wait()
    for k in range(planes):
        up = before_v[k].astype(jnp.float32)
        down = after_v[k].astype(jnp.float32)
        for t in range(tiles + 1):
            edges[k, t, EDGE:2 * EDGE, :] = up[t * EDGE:(t + 1) * EDGE]
            edges[k, t, 0:EDGE, :] = down[t * EDGE:(t + 1) * EDGE]

    m = tiles * nrows
    for k in range(planes):
        flank = edges[k]
        for side in range(2):
            lanes = slice(side * TILE_C, (side + 1) * TILE_C)
            pairs[k, 0:m, lanes] = main_v[k, side * nrows:m + side * nrows, :]
            pairs[k, m:m + tiles * TILE_R, lanes] = flank[side:tiles + side].reshape(
                tiles * TILE_R, TILE_C).astype(jnp.bfloat16)
    filt_copy.wait()

    @pl.loop(0, nfilt // 2)
    def _(c):
        cols = pl.ds(pl.multiple_of(c * 2 * TILE_C, 2 * TILE_C), 2 * TILE_C)
        filt = filt_v[:, cols]
        for k in range(planes):
            lhs = pairs[k]
            got = jnp.dot(jnp.concatenate([lhs, lhs], axis=1), filt, preferred_element_type=jnp.float32)
            for h in range(2):
                part = got[:, h * TILE_C:(h + 1) * TILE_C]
                ends = part[m:].reshape(tiles, TILE_R, TILE_C)
                field[2 * c + h, k, :, TILE_R:TILE_R + nrows, :] = part[:m].reshape(tiles, nrows, TILE_C)
                field[2 * c + h, k, :, 0:TILE_R, :] = ends
                field[2 * c + h, k, :, TILE_R + nrows:2 * TILE_R + nrows, :] = ends

    def tile(i, j):
        o = subcell_ref[i, j]
        oy = o // SUB
        fx = (o - oy * SUB) * 3
        wy = [table[oy, m] for m in range(NTAB)]
        y0, y1, y2 = wy[:4], wy[4:12], wy[12:20]
        shape = (TILE_R, TILE_C)
        zero = jnp.zeros(shape, jnp.float32)
        one = jnp.ones(shape, jnp.float32)
        dx, dy, a11, a12, a21, a22 = zero, zero, one, zero, zero, one
        for k in range(planes):
            def row(q, n):
                return field[fx + q, k, j, pl.ds(TILE_R + i * TILE_R + n, TILE_R), :]
            plain = [row(0, n) for n in range(-3, 5)]
            slope = [row(1, n) for n in range(-3, 5)]
            curve = [row(2, n) for n in range(-1, 3)]
            gx = sum(y0[b] * slope[b + 2] for b in range(4))
            xx = sum(y0[b] * curve[b] for b in range(4))
            xy = sum(y1[b] * slope[b] for b in range(8))
            gy = sum(y1[b] * plain[b] for b in range(8))
            yy = sum(y2[b] * plain[b] for b in range(8))
            lens = lens_ref[k]
            dx = dx + lens * gx
            dy = dy + lens * gy
            xx, xy, yy = lens * xx, lens * xy, lens * yy
            a11, a12, a21, a22 = (
                a11 - (xx * a11 + xy * a21),
                a12 - (xx * a12 + xy * a22),
                a21 - (xy * a11 + yy * a21),
                a22 - (xy * a12 + yy * a22),
            )
        at = pl.ds(pl.multiple_of(j * TILE_C, TILE_C), TILE_C)
        rs = slice(i * TILE_R, (i + 1) * TILE_R)
        deflect_ref[0, 0, rs, at] = dx
        deflect_ref[1, 0, rs, at] = dy
        for n, a in enumerate((a11, a12, a21, a22)):
            distort_ref[n, 0, rs, at] = a

    @pl.loop(0, tiles)
    def _(j):
        for i in range(nrows // TILE_R):
            tile(i, j)


def body(potential_stock, plane_pick, col_shift, mirror, subcell, lens_weight):
    held, rows, cols = potential_stock.shape
    peers = lax.axis_size("real")
    planes = plane_pick.shape[0]
    ncols = subcell.shape[1] * TILE_C
    out_tiles = -(-(ncols + 2 * EDGE) // TILE_C)
    erows = -(-(out_tiles * EDGE) // 16) * 16
    n = out_tiles * rows
    stock = potential_stock.reshape(held, rows // TILE_R, TILE_R, cols // TILE_C, TILE_C)
    stock = stock.transpose(0, 1, 3, 2, 4)
    vm = pl.BlockSpec(memory_space=pltpu.VMEM)
    sm = pl.BlockSpec(memory_space=pltpu.SMEM)
    anyw = pl.BlockSpec(memory_space=pl.ANY)
    bf = jnp.bfloat16
    dma = pltpu.SemaphoreType.DMA
    main, before, after = pl.pallas_call(
        exchange_kernel,
        out_shape=(
            jax.ShapeDtypeStruct((peers, held, n, TILE_C), bf),
            jax.ShapeDtypeStruct((peers, held, erows, TILE_C), bf),
            jax.ShapeDtypeStruct((peers, held, erows, TILE_C), bf),
        ),
        in_specs=[anyw, sm, vm, vm],
        out_specs=(anyw, anyw, anyw),
        scratch_shapes=[
            pltpu.VMEM(stock.shape, bf),
            pltpu.VMEM((n + rows, TILE_C), bf),
            pltpu.VMEM((peers, held, n, TILE_C), bf),
            pltpu.VMEM((2, erows, TILE_C), jnp.float32),
            pltpu.VMEM((peers, 2, held, erows, TILE_C), bf),
            pltpu.VMEM((peers, 1, planes), jnp.int32),
            pltpu.VMEM((peers, 1, planes), jnp.int32),
            pltpu.SMEM((peers, 1, planes), jnp.int32),
            pltpu.SMEM((peers, 1, planes), jnp.int32),
            dma((2, peers)), dma((2, peers)), dma((2,)), dma,
            dma((peers,)), dma((peers,)), dma((2, peers)), dma((2, peers)),
        ],
        compiler_params=pltpu.CompilerParams(collective_id=0, has_side_effects=True),
        name="exchange",
    )(stock, plane_pick, col_shift, mirror)
    f32 = jnp.float32
    nrows = subcell.shape[0] * TILE_R
    filt = jnp.asarray(column_filters())
    return pl.pallas_call(
        trace_kernel,
        out_shape=(
            jax.ShapeDtypeStruct((2, 1, nrows, ncols), f32),
            jax.ShapeDtypeStruct((4, 1, nrows, ncols), f32),
        ),
        in_specs=[sm, sm, sm, anyw, anyw, anyw, anyw],
        out_specs=(vm, vm),
        scratch_shapes=[
            pltpu.VMEM((planes, n, TILE_C), bf),
            pltpu.VMEM((planes, erows, TILE_C), bf),
            pltpu.VMEM((planes, erows, TILE_C), bf),
            pltpu.VMEM(filt.shape, bf),
            pltpu.VMEM((planes, ncols // TILE_C + 1, TILE_R, TILE_C), f32),
            pltpu.VMEM((planes, (ncols // TILE_C) * (nrows + TILE_R), 2 * TILE_C), bf),
            pltpu.VMEM((SUB * 3, planes, ncols // TILE_C, nrows + 2 * TILE_R, TILE_C), f32),
            pltpu.SMEM((SUB, NTAB), f32),
            dma((planes, 3)), dma,
        ],
        name="trace",
    )(plane_pick, subcell, lens_weight, filt, main, before, after)


def solution(mesh):
    return jax.shard_map(
        body,
        mesh=mesh,
        in_specs=(
            P("real", "sky", None),
            P(),
            P("real", None),
            P("real", None),
            P("sky", None),
            P(),
        ),
        out_specs=(P(None, "real", "sky", None), P(None, "real", "sky", None)),
        check_vma=False,
    )
```

```python
import jax
import jax.numpy as jnp
import numpy as np
from jax import lax
from jax.experimental import pallas as pl
from jax.experimental.pallas import tpu as pltpu
from jax.sharding import PartitionSpec as P

SUB = 4
TILE_R = 8
TILE_C = 128
EDGE = 4
MESH = pl.DeviceIdType.MESH

first_coef = (1.0 / 12.0, -8.0 / 12.0, 0.0, 8.0 / 12.0, -1.0 / 12.0)
second_coef = (-1.0 / 12.0, 16.0 / 12.0, -30.0 / 12.0, 16.0 / 12.0, -1.0 / 12.0)


def cubic(t):
    return (
        (-(t**3) + 2 * t**2 - t) / 2,
        (3 * t**3 - 5 * t**2 + 2) / 2,
        (-3 * t**3 + 4 * t**2 + t) / 2,
        (t**3 - t**2) / 2,
    )


def convolved(taps, coef):
    out = [0.0] * 8
    for a, w in enumerate(taps):
        for q, c in enumerate(coef):
            out[a + q] += w * c
    return out


def filter_table():
    rows = []
    for o in range(SUB):
        taps = cubic((o + 0.5) / SUB)
        rows.append(list(taps) + convolved(taps, first_coef) + convolved(taps, second_coef))
    return rows


TABLE = filter_table()
NTAB = 20
X_SCALE = 12288.0


def column_filters():
    full = np.zeros((2 * TILE_C, SUB, 3, TILE_C))
    out = np.arange(TILE_C)
    for o, row in enumerate(TABLE):
        for m in range(4):
            full[out + 3 + m, o, 0, out] = row[m] * X_SCALE
        for m in range(8):
            full[out + 1 + m, o, 1, out] = row[4 + m] * X_SCALE
            full[out + 1 + m, o, 2, out] = row[12 + m] * X_SCALE
    full = np.rint(full.reshape(2 * TILE_C, SUB * 3 * TILE_C)).astype(np.float32)
    high = full.astype(jnp.bfloat16)
    low = (full - high.astype(np.float32)).astype(jnp.bfloat16)
    return np.concatenate([high, low], axis=0)


def exchange_kernel(
    stock_ref, pick_ref, shift_ref, mirror_ref,
    main_ref, before_ref, after_ref,
    stock_t, tiles, send, edge32, esend, shifts_v, mirrors_v, shifts, mirrors,
    meta_send, meta_recv, local_sem, stock_sem, main_send, main_recv, edge_send, edge_recv,
):
    held, blocks, ntiles = stock_ref.shape[:3]
    rows, cols = blocks * TILE_R, ntiles * TILE_C
    out_tiles = main_ref.shape[2] // rows
    planes = pick_ref.shape[0]
    peers = lax.axis_size("real")
    strips = lax.axis_size("sky")
    me = lax.axis_index("real")
    strip = lax.axis_index("sky")
    above = lax.rem(strip + strips - 1, strips)
    below = lax.rem(strip + 1, strips)

    stock_copy = pltpu.make_async_copy(stock_ref, stock_t, stock_sem)
    stock_copy.start()
    barrier = pltpu.get_barrier_semaphore()
    for off in range(peers):
        r = lax.rem(me + off, peers)
        for s in (strip, above, below):
            if off == 0 and s is strip:
                continue
            pl.semaphore_signal(barrier, inc=1, device_id=(r, s), device_id_type=MESH)
    pl.semaphore_wait(barrier, 3 * peers - 1)

    def meta_copies(off):
        to = lax.rem(me + off, peers)
        return [
            pltpu.make_async_remote_copy(
                src_ref=src, dst_ref=dst.at[me], send_sem=meta_send.at[q, off],
                recv_sem=meta_recv.at[q, off], device_id=(to, strip), device_id_type=MESH)
            for q, (src, dst) in enumerate(((shift_ref, shifts_v), (mirror_ref, mirrors_v)))
        ]

    for off in range(1, peers):
        for copy in meta_copies(off):
            copy.start()
    own = [pltpu.make_async_copy(src, dst.at[me], local_sem.at[q])
           for q, (src, dst) in enumerate(((shift_ref, shifts_v), (mirror_ref, mirrors_v)))]
    for copy in own:
        copy.start()
    for copy in own:
        copy.wait()
    for off in range(1, peers):
        for copy in meta_copies(off):
            copy.wait()
    down = [pltpu.make_async_copy(src, dst, local_sem.at[q])
            for q, (src, dst) in enumerate(((shifts_v, shifts), (mirrors_v, mirrors)))]
    for copy in down:
        copy.start()
    for copy in down:
        copy.wait()

    lane_in = lax.broadcasted_iota(jnp.int32, (2 * TILE_C, TILE_C), 0)
    lane_out = lax.broadcasted_iota(jnp.int32, (2 * TILE_C, TILE_C), 1)

    def main_copy(off):
        to = lax.rem(me + off, peers)
        return pltpu.make_async_remote_copy(
            src_ref=send.at[off], dst_ref=main_ref.at[me], send_sem=main_send.at[off],
            recv_sem=main_recv.at[off], device_id=(to, strip), device_id_type=MESH)

    def edge_copies(off):
        to = lax.rem(me + off, peers)
        return [
            pltpu.make_async_remote_copy(
                src_ref=esend.at[off, 0], dst_ref=after_ref.at[me], send_sem=edge_send.at[0, off],
                recv_sem=edge_recv.at[0, off], device_id=(to, above), device_id_type=MESH),
            pltpu.make_async_remote_copy(
                src_ref=esend.at[off, 1], dst_ref=before_ref.at[me], send_sem=edge_send.at[1, off],
                recv_sem=edge_recv.at[1, off], device_id=(to, below), device_id_type=MESH),
        ]

    def cut(off):
        to = lax.rem(me + off, peers)
        for e in range(held):
            q = me * held + e
            shift = jnp.int32(0)
            turned = jnp.int32(0)
            for k in range(planes):
                hit = pick_ref[k] == q
                shift = jnp.where(hit, shifts[to, 0, k], shift)
                turned = jnp.where(hit, mirrors[to, 0, k], turned)
            step = 1 - 2 * turned
            start = turned * (cols + EDGE - 1 - shift) + (1 - turned) * (shift + cols - EDGE)
            start = lax.rem(start, cols)
            base = lax.div(start, TILE_C)
            inner = start - base * TILE_C
            for u in range(out_tiles + 1):
                at = lax.rem(base + step * u + ntiles, ntiles)
                for b in range(blocks):
                    tiles[u * rows + b * TILE_R:u * rows + (b + 1) * TILE_R, :] = stock_t[e, b, at]
            near = lane_in == inner + step * lane_out
            far = lane_in - TILE_C == inner + step * (lane_out - TILE_C)
            choose = ((near & (lane_in < TILE_C)) | (far & (lane_in >= TILE_C)))
            choose = choose.astype(jnp.float32).astype(jnp.bfloat16)
            n = out_tiles * rows
            pairs = jnp.concatenate([tiles[0:n, :], tiles[rows:n + rows, :]], axis=1)
            view = jnp.dot(pairs, choose, preferred_element_type=jnp.float32)
            send[off, e] = view.astype(jnp.bfloat16)
            for t in range(out_tiles):
                edge32[0, t * EDGE:(t + 1) * EDGE, :] = view[t * rows:t * rows + EDGE, :]
                edge32[1, t * EDGE:(t + 1) * EDGE, :] = view[(t + 1) * rows - EDGE:(t + 1) * rows, :]
            esend[off, 0, e] = edge32[0].astype(jnp.bfloat16)
            esend[off, 1, e] = edge32[1].astype(jnp.bfloat16)

    stock_copy.wait()
    edge32[...] = jnp.zeros_like(edge32)
    order = sorted(range(1, peers), key=lambda off: abs(2 * off - peers)) + [0]
    for off in order:
        cut(off)
        if off:
            main_copy(off).start()
        else:
            keep = pltpu.make_async_copy(send.at[0], main_ref.at[me], local_sem.at[0])
            keep.start()
        for copy in edge_copies(off):
            copy.start()
    keep.wait()
    for off in order:
        if off:
            main_copy(off).wait()
        for copy in edge_copies(off):
            copy.wait()


def trace_kernel(
    pick_ref, subcell_ref, lens_ref, filt_ref, main_ref, before_ref, after_ref,
    deflect_ref, distort_ref,
    main_v, before_v, after_v, filt_v, edges, pairs, field_a, field_b, table, sems, filt_sem,
):
    planes = pick_ref.shape[0]
    held = main_ref.shape[1]
    nrows = deflect_ref.shape[2]
    ncols = deflect_ref.shape[3]
    tiles = ncols // TILE_C
    nfilt = filt_ref.shape[1] // TILE_C

    filt_copy = pltpu.make_async_copy(filt_ref, filt_v, filt_sem)
    filt_copy.start()
    copies = []
    for k in range(planes):
        group = pick_ref[k] // held
        e = lax.rem(pick_ref[k], held)
        copies.append([
            pltpu.make_async_copy(src.at[group, e], dst.at[k], sems.at[k, q])
            for q, (src, dst) in enumerate(
                ((main_ref, main_v), (before_ref, before_v), (after_ref, after_v)))
        ])
        for copy in copies[k]:
            copy.start()
    for o in range(SUB):
        for m in range(NTAB):
            table[o, m] = jnp.float32(TABLE[o][m] / X_SCALE)
    for k in range(planes):
        for copy in copies[k]:
            copy.wait()
    for k in range(planes):
        up = before_v[k].astype(jnp.float32)
        down = after_v[k].astype(jnp.float32)
        for t in range(tiles + 1):
            edges[k, t, EDGE:2 * EDGE, :] = up[t * EDGE:(t + 1) * EDGE]
            edges[k, t, 0:EDGE, :] = down[t * EDGE:(t + 1) * EDGE]

    m = tiles * nrows
    for k in range(planes):
        flank = edges[k]
        for side in range(2):
            lanes = slice(side * TILE_C, (side + 1) * TILE_C)
            pairs[k, 0:m, lanes] = main_v[k, side * nrows:m + side * nrows, :]
            pairs[k, m:m + tiles * TILE_R, lanes] = flank[side:tiles + side].reshape(
                tiles * TILE_R, TILE_C).astype(jnp.bfloat16)
    filt_copy.wait()

    span = field_a.shape[2]
    fields = (field_a, field_b)

    def filter_pair(g, c):
        field = fields[g % 2]
        mains = slice(g * span * nrows, (g + 1) * span * nrows)
        flanks = slice(m + g * span * TILE_R, m + (g + 1) * span * TILE_R)
        lhs = jnp.concatenate(
            [pairs[k, mains, :] for k in range(planes)] + [pairs[k, flanks, :] for k in range(planes)], axis=0)
        got = jnp.dot(
            jnp.concatenate([lhs, lhs], axis=1), filt_v[:, 2 * c * TILE_C:2 * (c + 1) * TILE_C],
            preferred_element_type=jnp.float32)
        for h in range(2):
            part = got[:, h * TILE_C:(h + 1) * TILE_C]
            body_rows = part[:planes * span * nrows].reshape(planes, span, nrows, TILE_C)
            ends = part[planes * span * nrows:].reshape(planes, span, TILE_R, TILE_C)
            field[2 * c + h, :, :, TILE_R:TILE_R + nrows, :] = body_rows
            field[2 * c + h, :, :, 0:TILE_R, :] = ends
            field[2 * c + h, :, :, TILE_R + nrows:2 * TILE_R + nrows, :] = ends

    def tile(i, j):
        field, jj = fields[(j // span) % 2], j % span
        o = subcell_ref[i, j]
        oy = o // SUB
        fx = (o - oy * SUB) * 3
        wy = [table[oy, m] for m in range(NTAB)]
        y0, y1, y2 = wy[:4], wy[4:12], wy[12:20]
        shape = (TILE_R, TILE_C)
        zero = jnp.zeros(shape, jnp.float32)
        one = jnp.ones(shape, jnp.float32)
        dx, dy, a11, a12, a21, a22 = zero, zero, one, zero, zero, one
        for k in range(planes):
            def row(q, n):
                return field[fx + q, k, jj, pl.ds(TILE_R + i * TILE_R + n, TILE_R), :]
            plain = [row(0, n) for n in range(-3, 5)]
            slope = [row(1, n) for n in range(-3, 5)]
            curve = [row(2, n) for n in range(-1, 3)]
            gx = sum(y0[b] * slope[b + 2] for b in range(4))
            xx = sum(y0[b] * curve[b] for b in range(4))
            xy = sum(y1[b] * slope[b] for b in range(8))
            gy = sum(y1[b] * plain[b] for b in range(8))
            yy = sum(y2[b] * plain[b] for b in range(8))
            lens = lens_ref[k]
            dx = dx + lens * gx
            dy = dy + lens * gy
            xx, xy, yy = lens * xx, lens * xy, lens * yy
            a11, a12, a21, a22 = (
                a11 - (xx * a11 + xy * a21),
                a12 - (xx * a12 + xy * a22),
                a21 - (xy * a11 + yy * a21),
                a22 - (xy * a12 + yy * a22),
            )
        at = slice(j * TILE_C, (j + 1) * TILE_C)
        rs = slice(i * TILE_R, (i + 1) * TILE_R)
        deflect_ref[0, 0, rs, at] = dx
        deflect_ref[1, 0, rs, at] = dy
        for n, a in enumerate((a11, a12, a21, a22)):
            distort_ref[n, 0, rs, at] = a

    groups = tiles // span
    npairs = nfilt // 2
    for c in range(npairs):
        filter_pair(0, c)
    for g in range(groups):
        todo = [(i, g * span + jj) for jj in range(span) for i in range(nrows // TILE_R)]
        each = -(-len(todo) // npairs)
        for c in range(npairs):
            if g + 1 < groups:
                filter_pair(g + 1, c)
            for i, j in todo[c * each:(c + 1) * each]:
                tile(i, j)


def body(potential_stock, plane_pick, col_shift, mirror, subcell, lens_weight):
    held, rows, cols = potential_stock.shape
    peers = lax.axis_size("real")
    planes = plane_pick.shape[0]
    ncols = subcell.shape[1] * TILE_C
    out_tiles = -(-(ncols + 2 * EDGE) // TILE_C)
    erows = -(-(out_tiles * EDGE) // 16) * 16
    n = out_tiles * rows
    stock = potential_stock.reshape(held, rows // TILE_R, TILE_R, cols // TILE_C, TILE_C)
    stock = stock.transpose(0, 1, 3, 2, 4)
    vm = pl.BlockSpec(memory_space=pltpu.VMEM)
    sm = pl.BlockSpec(memory_space=pltpu.SMEM)
    anyw = pl.BlockSpec(memory_space=pl.ANY)
    bf = jnp.bfloat16
    dma = pltpu.SemaphoreType.DMA
    main, before, after = pl.pallas_call(
        exchange_kernel,
        out_shape=(
            jax.ShapeDtypeStruct((peers, held, n, TILE_C), bf),
            jax.ShapeDtypeStruct((peers, held, erows, TILE_C), bf),
            jax.ShapeDtypeStruct((peers, held, erows, TILE_C), bf),
        ),
        in_specs=[anyw, sm, vm, vm],
        out_specs=(anyw, anyw, anyw),
        scratch_shapes=[
            pltpu.VMEM(stock.shape, bf),
            pltpu.VMEM((n + rows, TILE_C), bf),
            pltpu.VMEM((peers, held, n, TILE_C), bf),
            pltpu.VMEM((2, erows, TILE_C), jnp.float32),
            pltpu.VMEM((peers, 2, held, erows, TILE_C), bf),
            pltpu.VMEM((peers, 1, planes), jnp.int32),
            pltpu.VMEM((peers, 1, planes), jnp.int32),
            pltpu.SMEM((peers, 1, planes), jnp.int32),
            pltpu.SMEM((peers, 1, planes), jnp.int32),
            dma((2, peers)), dma((2, peers)), dma((2,)), dma,
            dma((peers,)), dma((peers,)), dma((2, peers)), dma((2, peers)),
        ],
        compiler_params=pltpu.CompilerParams(collective_id=0, has_side_effects=True),
        name="exchange",
    )(stock, plane_pick, col_shift, mirror)
    f32 = jnp.float32
    nrows = subcell.shape[0] * TILE_R
    tiles = ncols // TILE_C
    span = next(d for d in (4, 3, 2, 1) if tiles % d == 0)
    filt = jnp.asarray(column_filters())
    return pl.pallas_call(
        trace_kernel,
        out_shape=(
            jax.ShapeDtypeStruct((2, 1, nrows, ncols), f32),
            jax.ShapeDtypeStruct((4, 1, nrows, ncols), f32),
        ),
        in_specs=[sm, sm, sm, anyw, anyw, anyw, anyw],
        out_specs=(vm, vm),
        scratch_shapes=[
            pltpu.VMEM((planes, n, TILE_C), bf),
            pltpu.VMEM((planes, erows, TILE_C), bf),
            pltpu.VMEM((planes, erows, TILE_C), bf),
            pltpu.VMEM(filt.shape, bf),
            pltpu.VMEM((planes, ncols // TILE_C + 1, TILE_R, TILE_C), f32),
            pltpu.VMEM((planes, (ncols // TILE_C) * (nrows + TILE_R), 2 * TILE_C), bf),
            pltpu.VMEM((SUB * 3, planes, span, nrows + 2 * TILE_R, TILE_C), f32),
            pltpu.VMEM((SUB * 3, planes, span, nrows + 2 * TILE_R, TILE_C), f32),
            pltpu.SMEM((SUB, NTAB), f32),
            dma((planes, 3)), dma,
        ],
        name="trace",
    )(plane_pick, subcell, lens_weight, filt, main, before, after)


def solution(mesh):
    return jax.shard_map(
        body,
        mesh=mesh,
        in_specs=(
            P("real", "sky", None),
            P(),
            P("real", None),
            P("real", None),
            P("sky", None),
            P(),
        ),
        out_specs=(P(None, "real", "sky", None), P(None, "real", "sky", None)),
        check_vma=False,
    )
```
